1024 devices in a mesh: doc: 32 (over z), fsdp: 32 (over x, y, core).
Axes of the slice: x: 4, y: 4, z: 32, core: 2. Of those that a mesh axis runs over, the one named last changes fastest.
Arguments:
- tokens_in: bfloat16 [32, 256, 4096], P('doc'), may hold values from -6 to 6
- mix_in: bfloat16 [32, 256, 8192], P('doc', None, 'fsdp'), may hold values from -6 to 6
- step_size: float32 [32, 256, 128], P('doc', None, 'fsdp'), may hold values from 0.0025 to 0.03
- doc_ids: int32 [32, 256], P('doc'), may hold values from 0 to 3, never falling along the last dimension, each value on 1 to 128 neighbouring positions
- out_grad: bfloat16 [32, 256, 8192], P('doc', None, 'fsdp'), may hold values from -6 to 6
- proj_weight: bfloat16 [4096, 256], P('fsdp'), may hold values from -0.046875 to 0.046875
- conv_weight: float32 [4, 8192], P(None, 'fsdp'), may hold values from -3 to 3
- decay_rate: float32 [128], P('fsdp'), may hold values from 0.02 to 2.5
- carried_state: bfloat16 [32, 128, 64, 128], P(None, 'fsdp', 'doc'), may hold values from -3 to 3
- carried_conv: bfloat16 [32, 3, 128, 64], P(None, None, 'fsdp', 'doc'), may hold values from -6 to 6
- carry_from: int32 [32], replicated, may hold values from -1 to 31, as said below
Outputs:
- grad_proj: float32 [4096, 256], P(('doc', 'fsdp'))
- grad_state: bfloat16 [32, 128, 64, 128], P(None, 'fsdp', 'doc')
- grad_conv: bfloat16 [32, 3, 128, 64], P(None, None, 'fsdp', 'doc')
The draws below stay inside these ranges and needn't reach their ends.
Inputs may be any that keep to these rules, and one draw needn't show every extreme that they name: `carry_from`: each row names the slot of the previous window that its first document continues, or -1 if it starts fresh; no slot is named by two rows.
All inputs are finite; a program needn't handle non-finite values.
Results may differ from the reference program's by a relative error of at most 0.007.
Values may be sent and summed in bfloat16 or wider, within the bound.
No kernel may reach another device: no remote copies, remote signals or barrier semaphores. Data moves between devices by JAX's collectives and lax.ppermute only.
A program may use at most 32 MiB of HBM per device.

```python
import math
import jax
import jax.numpy as jnp
import numpy as np
from jax import lax

D = 4096
LOCAL_HEADS = 128
P_SIZE = 64
N = 128
K = 4
ROW_TOKENS = 256
PACKED_ROWS = 32
DI = 8192


def draw_step_size(key, part):
    row_random_key, token_random_key = jax.random.split(key, 2)
    row_factor_scale = jnp.exp(jax.random.uniform(row_random_key, (PACKED_ROWS, 1, 1), jnp.float32, math.log(0.5), math.log(2.0)))
    token_factor_scale = jax.random.uniform(token_random_key, (PACKED_ROWS, ROW_TOKENS, LOCAL_HEADS), jnp.float32, 0.5, 1.5)
    return (0.01 * row_factor_scale * token_factor_scale).astype(jnp.float32)


def draw_decay_rate(key, part):
    key_base = jax.random.fold_in(key, 0)
    base_rate = jnp.exp(jax.random.uniform(key_base, (LOCAL_HEADS,), jnp.float32, math.log(0.08), math.log(2.5)))
    return base_rate.astype(jnp.float32)


def draw_carry_from(key, part):
    ordering = jax.random.permutation(key, PACKED_ROWS).astype(jnp.int32)
    coin_flip = jax.random.randint(jax.random.fold_in(key, 7), (PACKED_ROWS,), 0, 4)
    position = jnp.arange(PACKED_ROWS, dtype=jnp.int32)
    target = jnp.where(ordering[0] == PACKED_ROWS - 1, 1, 0)
    dropped = ((coin_flip == 0) | (position == target)) & (ordering != PACKED_ROWS - 1)
    return jnp.where(dropped, -1, ordering).astype(jnp.int32)


def spiked(values, key, source, target, shards_of, factor):
    owner, partner = [(jnp.arange(values.shape[axis_at]) // (values.shape[axis_at] // shards_of)).reshape([-1 if axis == axis_at else 1 for axis in range(values.ndim)]) for axis_at in (source, target)]
    chosen = jax.random.permutation(key, shards_of)[partner]
    strong = (owner == chosen) | (owner == (partner + shards_of // 2) % shards_of)
    return jnp.where(strong, factor * values, values)


def block_scale(rng, shape, cuts, low, top_value):
    factor_of = 1.0
    for dim, blocks in cuts:
        heights = jax.random.uniform(jax.random.fold_in(jax.random.fold_in(rng, 6), dim), (blocks,), jnp.float32, low / len(cuts), top_value / len(cuts))
        factor_of = factor_of * jnp.repeat(jnp.exp(heights), shape[dim] // blocks).reshape((-1,) + (1,) * (len(shape) - 1 - dim))
    return factor_of


def profile(amount, total, reach, lean):
    loads = [(1 << 20) // math.isqrt(standing ** lean) + 1 for standing in range(2, amount + 1)]
    surplus, counts = total - reach - (amount - 1), [1] * (amount - 1)
    while surplus > 0:
        movable = [i for i in range(amount - 1) if counts[i] < reach]
        mass, left = sum([loads[i] for i in movable]), surplus
        for i in movable:
            addition = min(reach - counts[i], max(1, left * loads[i] // mass), surplus)
            counts[i] = counts[i] + addition
            surplus = surplus - addition
    return np.array([reach] + counts)


def ragged(own_key, amount, total, limit, skew):
    if amount == 2:
        one = jax.random.randint(own_key, (), max(1, total - limit), min(limit, total - 1) + 1)
        return jnp.stack([one, total - one])
    sizes = jnp.asarray(profile(amount, total, limit, skew), jnp.int32)
    pairs = (amount - 1) // 2
    giver, taker = sizes[1:1 + 2 * pairs:2], sizes[2:2 + 2 * pairs:2]
    margin = jnp.minimum(giver - 1, limit - taker)
    moved = jax.random.randint(jax.random.fold_in(own_key, 1), (pairs,), 0, 1 << 20) % (margin + 1)
    sizes = sizes.at[1:1 + 2 * pairs:2].set(giver - moved).at[2:2 + 2 * pairs:2].set(taker + moved)
    return sizes[jax.random.permutation(jax.random.fold_in(own_key, 2), amount)]


def normal_values(stream_key, shape, scale, most, pieces=(), kind=jnp.bfloat16):
    result = jax.random.normal(stream_key, shape, jnp.float32) * scale
    if len(pieces) > 0:
        result = block_scale(stream_key, shape, pieces, -0.22, 0.18) * result
    return jnp.clip(result, min=-most, max=most).astype(kind)


def noise_with(own_key, extent, scale, bound, shards, heavy, kind=jnp.bfloat16):
    result = scale * jax.random.normal(own_key, extent, jnp.float32)
    if shards:
        result = result * block_scale(own_key, extent, shards, -0.22, 0.18)
    return jnp.clip(spiked(result, jax.random.fold_in(own_key, 3), *heavy), -bound, bound).astype(kind)


def setup_inputs(seed: int = 0) -> dict:
    splits = jax.random.split(jax.random.key(seed), 12)
    tokens_in = noise_with(splits[0], (PACKED_ROWS, ROW_TOKENS, D), 1.0, 6.0, ((0, 32),), (0, 2, 32, 2.75))
    mix_in = normal_values(splits[1], (PACKED_ROWS, ROW_TOKENS, DI), 1.0, 6.0, ((0, 32), (2, 32)))
    step_size = draw_step_size(jax.random.fold_in(splits[11], 71), 0)
    doc_ids = jax.vmap(lambda own: jnp.searchsorted(jnp.cumsum(ragged(own, 4, ROW_TOKENS, ROW_TOKENS // 2, 0)), jnp.arange(ROW_TOKENS), side="right"))(jax.random.split(splits[3], PACKED_ROWS)).reshape((PACKED_ROWS, ROW_TOKENS)).astype(jnp.int32)
    out_grad = normal_values(splits[4], (PACKED_ROWS, ROW_TOKENS, DI), 1.0, 6.0, ((0, 32), (2, 32)))
    proj_weight = normal_values(splits[5], (D, 2 * N), (4 * D) ** -0.5, 0.046875, ((0, 32),))
    conv_weight = normal_values(splits[6], (K, DI), 0.5, 3.0, ((1, 32),), jnp.float32)
    decay_rate = draw_decay_rate(jax.random.fold_in(splits[11], 71), 0)
    carried_state = normal_values(splits[8], (PACKED_ROWS, LOCAL_HEADS, P_SIZE, N), 0.5, 3.0, ((1, 32), (2, 32)))
    carried_conv = normal_values(splits[9], (PACKED_ROWS, K - 1, LOCAL_HEADS, P_SIZE), 1.0, 6.0, ((2, 32), (3, 32)))
    carry_from = draw_carry_from(jax.random.fold_in(splits[11], 71), 0)
    return dict(tokens_in=tokens_in, mix_in=mix_in, step_size=step_size, doc_ids=doc_ids, out_grad=out_grad, proj_weight=proj_weight, conv_weight=conv_weight, decay_rate=decay_rate, carried_state=carried_state, carried_conv=carried_conv, carry_from=carry_from)


def silu_slope(value):
    sigmoid_value = jax.nn.sigmoid(value)
    return sigmoid_value * (1.0 + value * (1.0 - sigmoid_value))


def conv_masks(seg_row, tap_count):
    length = seg_row.shape[0]
    opening = seg_row == seg_row[0]
    tap_masks = []
    for offset in range(tap_count):
        earlier = jnp.concatenate([jnp.full((offset,), -1, jnp.int32), seg_row[: length - offset].astype(jnp.int32)])
        inside = jnp.arange(length) >= offset
        tap_masks.append(jnp.where(inside, earlier == seg_row, opening))
    return opening, tap_masks


def row_pass(coeff, mix_row, step_row, seg_row, grad_rows, state_zero, conv_zero, conv_weight, decay_rate):
    length, channels = mix_row.shape
    head_count = step_row.shape[1]
    head_dim = channels // head_count
    tap_count = conv_weight.shape[0]
    nstate = coeff.shape[1] // 2
    opening, tap_masks = conv_masks(seg_row, tap_count)
    extended = jnp.concatenate([conv_zero, mix_row], axis=0).astype(jnp.float32)
    preact = jnp.zeros((length, channels), jnp.float32)
    for offset in range(tap_count):
        window = extended[tap_count - 1 - offset: tap_count - 1 - offset + length]
        preact = preact + jnp.where(tap_masks[offset][:, None], conv_weight[offset][None, :] * window, 0.0)
    mixed_rows = jax.nn.silu(preact).astype(jnp.bfloat16)
    values = (step_row[:, :, None] * mixed_rows.reshape(length, head_count, head_dim).astype(jnp.float32)).astype(jnp.bfloat16)
    write_coeff = coeff[:, :nstate]
    read_coeff = coeff[:, nstate:]
    scores = jnp.dot(read_coeff, write_coeff.T, preferred_element_type=jnp.float32)
    log_decay = jnp.cumsum(-(decay_rate[None, :] * step_row), axis=0).T
    lower = jnp.arange(length)[:, None] >= jnp.arange(length)[None, :]
    allowed = lower & (seg_row[:, None] == seg_row[None, :])
    spread = log_decay[:, :, None] - log_decay[:, None, :]
    decays = jnp.where(allowed[None], jnp.exp(jnp.where(allowed[None], spread, 0.0)), 0.0)
    edge_weight = jnp.where(opening[None, :], jnp.exp(log_decay), 0.0)
    weighted = (decays * scores[None]).astype(jnp.bfloat16)
    grad_heads = grad_rows.reshape(length, head_count, head_dim)
    values_grad = jnp.einsum("hts,thp->shp", weighted.astype(jnp.float32), grad_heads.astype(jnp.float32))
    products = jnp.einsum("thp,shp->hts", grad_heads.astype(jnp.float32), values.astype(jnp.float32))
    score_grad = jnp.sum(decays * products, axis=0)
    carried = jnp.einsum("thp,hpn->thn", grad_heads.astype(jnp.float32), state_zero.astype(jnp.float32))
    read_grad = jnp.dot(score_grad, write_coeff.astype(jnp.float32), precision=lax.Precision.HIGHEST)
    read_grad = read_grad + jnp.sum(edge_weight.T[:, :, None] * carried, axis=1)
    write_grad = jnp.dot(score_grad.T, read_coeff.astype(jnp.float32), precision=lax.Precision.HIGHEST)
    scaled = edge_weight.T[:, :, None] * grad_heads.astype(jnp.float32)
    state_grad = jnp.einsum("thp,tn->hpn", scaled, read_coeff.astype(jnp.float32), precision=lax.Precision.HIGHEST)
    mixed_grad = (values_grad * step_row[:, :, None]).reshape(length, channels)
    preact_grad = mixed_grad * silu_slope(preact)
    conv_rows = []
    for index_row in range(tap_count - 1):
        running = jnp.zeros((channels,), jnp.float32)
        for offset in range(tap_count - 1 - index_row, tap_count):
            position = index_row - (tap_count - 1) + offset
            running = running + jnp.where(opening[position], conv_weight[offset] * preact_grad[position], 0.0)
        conv_rows.append(running)
    conv_grad = jnp.stack(conv_rows)
    return jnp.concatenate([write_grad, read_grad], axis=1), state_grad, conv_grad


def reference(tokens_in, mix_in, step_size, doc_ids, out_grad, proj_weight, conv_weight, decay_rate, carried_state, carried_conv, carry_from):
    slot_count = carried_state.shape[0]
    row_total = tokens_in.shape[0]
    model_width = tokens_in.shape[2]
    channels = mix_in.shape[2]
    tap_count = conv_weight.shape[0]

    def one_row(running, index_row):
        source = carry_from[index_row]
        usable = source >= 0
        clipped = jnp.maximum(source, 0).astype(jnp.int32)
        state_zero = jnp.where(usable, carried_state[clipped], jnp.zeros_like(carried_state[0]))
        conv_zero = jnp.where(usable, carried_conv[clipped], jnp.zeros_like(carried_conv[0])).reshape(tap_count - 1, channels)
        coeff = jnp.dot(tokens_in[index_row], proj_weight, preferred_element_type=jnp.float32).astype(jnp.bfloat16)
        coeff_grad, state_grad, conv_grad = row_pass(coeff, mix_in[index_row], step_size[index_row], doc_ids[index_row], out_grad[index_row], state_zero, conv_zero, conv_weight, decay_rate)
        running = running + jnp.einsum("tj,tn->jn", tokens_in[index_row].astype(jnp.float32), coeff_grad, precision=lax.Precision.HIGHEST)
        return running, (state_grad.astype(jnp.bfloat16), conv_grad.astype(jnp.bfloat16))

    grad_proj, (state_grads, conv_grads) = lax.scan(one_row, jnp.zeros((model_width, proj_weight.shape[1]), jnp.float32), jnp.arange(row_total, dtype=jnp.int32))
    picker = (carry_from[:, None] == jnp.arange(slot_count, dtype=jnp.int32)[None, :]).astype(jnp.float32)
    grad_state = jnp.dot(picker.T, state_grads.reshape(row_total, -1).astype(jnp.float32), precision=lax.Precision.HIGHEST)
    grad_state = grad_state.astype(jnp.bfloat16).reshape(carried_state.shape)
    grad_conv = jnp.dot(picker.T, conv_grads.reshape(row_total, -1).astype(jnp.float32), precision=lax.Precision.HIGHEST)
    grad_conv = grad_conv.astype(jnp.bfloat16).reshape(carried_conv.shape)
    return grad_proj, grad_state, grad_conv
```

```python
import jax
import jax.numpy as jnp
from jax import lax
from jax.experimental import pallas as pl
from jax.experimental.pallas import tpu as pltpu
from jax.sharding import PartitionSpec as P

INTERPRET = False
F32 = jnp.float32
BF16 = jnp.bfloat16


def iota(shape, dim):
    return lax.broadcasted_iota(jnp.int32, shape, dim)


def one_hot(condition):
    return jnp.where(condition, 1.0, 0.0).astype(BF16)


def dot(a, b):
    return jnp.dot(a, b, preferred_element_type=F32)


def dot_nt(a, b, precision=None):
    return lax.dot_general(
        a, b, (((1,), (1,)), ((), ())), precision=precision, preferred_element_type=F32
    )


def halves(value):
    high = value.astype(BF16)
    return high, (value - high.astype(F32)).astype(BF16)


def call(body, out_shape, in_specs, scratch=()):
    vmem = pl.BlockSpec(memory_space=pltpu.VMEM)
    smem = pl.BlockSpec(memory_space=pltpu.SMEM)
    many = isinstance(out_shape, tuple)
    return pl.pallas_call(
        body,
        out_shape=out_shape,
        in_specs=[smem if spec == "s" else vmem for spec in in_specs],
        out_specs=tuple(vmem for _ in out_shape) if many else vmem,
        scratch_shapes=list(scratch),
        interpret=INTERPRET,
    )


def shaped(shape, kind):
    return jax.ShapeDtypeStruct(shape, kind)


def pick_body(carry_ref, slots_ref, picked_ref):
    for r in range(picked_ref.shape[0]):
        source = carry_ref[r]
        row = slots_ref[jnp.maximum(source, 0)]
        picked_ref[r] = jnp.where(source >= 0, row, jnp.zeros_like(row))


def turn_body(weight_ref, turned_ref):
    rows, columns = weight_ref.shape
    turned = weight_ref[...].astype(F32).T
    turned_ref[...] = turned.reshape(columns // 8, 8, rows).astype(BF16)


def coeff_body(weight_ref, tokens_ref, copies_ref):
    parts = weight_ref.shape[0]
    weight = jnp.concatenate([weight_ref[i] for i in range(parts)], axis=1)
    column = dot_nt(weight, tokens_ref[...]).astype(BF16)
    for i in range(parts):
        copies_ref[i] = column


def row_body(
    decay_ref,
    coeff_ref,
    mix_ref,
    step_ref,
    doc_ref,
    grad_ref,
    tap_ref,
    start_ref,
    coeff_grad_ref,
    state_ref,
    conv_ref,
    ext,
    doc_ext,
):
    length, channels = mix_ref.shape
    heads = step_ref.shape[1]
    head_dim = channels // heads
    taps = tap_ref.shape[0]
    docs = start_ref.shape[0]
    part_p = head_dim // docs
    rows_in = heads * part_p
    nstate = start_ref.shape[2]
    square = (length, channels)

    start = start_ref[...].astype(F32)
    state_in = start[:, :rows_in].reshape(channels, nstate).astype(BF16)
    conv_in = jnp.sum(start[:, rows_in:], axis=1).astype(BF16)
    chan = iota((channels, channels), 0)
    other = iota((channels, channels), 1)
    place = (
        ((chan % head_dim) // part_p) * rows_in + (chan // head_dim) * part_p + chan % part_p
    )
    to_natural = one_hot(place == other)
    place_t = (
        ((other % head_dim) // part_p) * rows_in + (other // head_dim) * part_p + other % part_p
    )
    to_parts = one_hot(place_t == chan)
    state_zero = dot(to_natural, state_in).astype(BF16)
    lane_chan = iota((nstate, channels), 1)
    lane = iota((nstate, channels), 0)
    lane_of = (lane_chan // head_dim) * part_p + lane_chan % part_p
    owner = (iota((docs, channels), 1) % head_dim) // part_p == iota((docs, channels), 0)
    sub = iota((8, channels), 0)
    head_rows = jnp.zeros((8, channels), F32)
    for k in range(taps - 1):
        spread_row = dot(conv_in, one_hot(lane == k * rows_in + lane_of))
        line = jnp.sum(jnp.where(owner, spread_row, 0.0), axis=0, keepdims=True)
        head_rows = jnp.where(sub == 8 - (taps - 1) + k, line, head_rows)

    doc_row = doc_ref[...]
    doc_turned = jnp.broadcast_to(doc_row.astype(F32), (128, length)).T
    doc_col = jnp.concatenate([doc_turned] * (channels // 128), axis=1)
    doc_first = doc_row[0:1, 0:1].astype(F32)
    opening = doc_col == doc_first
    doc_ext[0:8] = jnp.broadcast_to(doc_first, (8, channels))
    doc_ext[8:] = doc_col

    ext[0:8] = head_rows
    ext[8:] = mix_ref[...].astype(F32)
    preact = jnp.zeros(square, F32)
    for k in range(taps):
        same = doc_ext[8 - k : 8 - k + length] == doc_col
        term = tap_ref[k : k + 1] * ext[8 - k : 8 - k + length]
        preact = preact + jnp.where(same, term, 0.0)
    head_of = iota(square, 1) // head_dim
    step = jnp.broadcast_to(step_ref[:, 0:1], square)
    rate = jnp.where(head_of[0:1] == 0, decay_ref[0], 0.0)
    for h in range(1, heads):
        step = jnp.where(head_of == h, step_ref[:, h : h + 1], step)
        rate = jnp.where(head_of[0:1] == h, decay_ref[h], rate)
    gate = 1.0 / (1.0 + jnp.exp(-preact))
    mixed = (preact * gate).astype(BF16).astype(F32)
    values = (step * mixed).astype(BF16)

    time_row = iota((length, length), 0)
    time_col = iota((length, length), 1)
    lower = time_row >= time_col
    lower_one = one_hot(lower)
    change = -(rate * step)
    first = change.astype(BF16)
    rest = change - first.astype(F32)
    second, third = halves(rest)
    log_decay = dot(lower_one, first) + (dot(lower_one, second) + dot(lower_one, third))
    log_turned = log_decay.T
    allowed = lower & (doc_col == doc_row.astype(F32))
    grad = grad_ref[...]
    grad_wide = grad.astype(F32)
    score_grad = jnp.zeros((length, length), F32)
    for h in range(heads):
        own = jnp.where(head_of == h, grad_wide, 0.0).astype(BF16)
        products = dot_nt(own, values)
        column = log_decay[:, h * head_dim : h * head_dim + 1]
        spread = column - log_turned[h * head_dim : h * head_dim + 1]
        decays = jnp.where(allowed, jnp.exp(jnp.where(allowed, spread, 0.0)), 0.0)
        score_grad = score_grad + decays * products

    coeff = coeff_ref[...].astype(F32).reshape(2 * nstate, length)
    write_turned = coeff[:nstate]
    read_turned = coeff[nstate:]
    write = write_turned.T.astype(BF16)
    read = read_turned.T.astype(BF16)
    read_turned = read_turned.astype(BF16)

    edge = jnp.where(opening, jnp.exp(log_decay), 0.0)
    scaled_high, scaled_low = halves(edge * grad_wide)
    score_high, score_low = halves(score_grad)
    read_grad = dot(score_high, write) + dot(score_low, write)
    read_grad = read_grad + dot(scaled_high, state_zero) + dot(scaled_low, state_zero)
    write_grad = dot(read_turned, score_high) + dot(read_turned, score_low)
    coeff_grad = jnp.concatenate([write_grad, read_grad.T], axis=0)
    coeff_grad_ref[...] = coeff_grad.reshape(coeff_grad_ref.shape).astype(BF16)
    state_grad = dot(read_turned, scaled_high) + dot(read_turned, scaled_low)
    state_grad = state_grad.T.astype(BF16)
    state_ref[...] = dot(to_parts, state_grad).reshape(state_ref.shape).astype(BF16)

    scores = dot_nt(read, write[0:16])
    time = iota(square, 0)
    pre_grads = []
    for s in range(taps - 1):
        inside = (time >= s) & (doc_col == doc_col[s : s + 1])
        spread = jnp.where(inside, log_decay - log_decay[s : s + 1], 0.0)
        weighted = jnp.where(inside, jnp.exp(spread), 0.0) * scores[:, s : s + 1]
        weighted = weighted.astype(BF16).astype(F32)
        value_grad = jnp.sum(weighted * grad_wide, axis=0, keepdims=True)
        g = gate[s : s + 1]
        slope = g * (1.0 + preact[s : s + 1] * (1.0 - g))
        pre_grad = value_grad * step[s : s + 1] * slope
        pre_grads.append(jnp.where(opening[s : s + 1], pre_grad, 0.0))
    lines = jnp.zeros((docs, nstate), F32)
    for j in range(taps - 1):
        line = jnp.zeros((1, channels), F32)
        for k in range(taps - 1 - j, taps):
            line = line + tap_ref[k : k + 1] * pre_grads[j - (taps - 1) + k]
        line = jnp.where(owner, jnp.broadcast_to(line, (docs, channels)), 0.0).astype(BF16)
        lines = lines + dot_nt(line, one_hot(lane == j * rows_in + lane_of))
    for d in range(docs):
        conv_ref[d] = jnp.broadcast_to(lines[d : d + 1], (8, nstate)).astype(BF16)


def project_body(got_ref, tokens_ref, state_ref, conv_ref, out_ref):
    parts = out_ref.shape[0]
    rows = got_ref.shape[1]
    summed = jnp.sum(got_ref[...].astype(F32), axis=0)
    high = summed.astype(BF16).astype(F32)
    both = jnp.concatenate([high, summed - high], axis=0).astype(BF16)
    partial = dot(both, tokens_ref[...])
    partial = (partial[:rows] + partial[rows:]).astype(BF16)
    width = partial.shape[1] // parts
    for d in range(parts):
        out_ref[d, 0:8] = state_ref[d]
        out_ref[d, 8:16] = partial[:, d * width : (d + 1) * width]
        out_ref[d, 16:24] = conv_ref[d]


def place_body(carry_ref, got_ref, state_ref, conv_ref, copies_ref):
    rows = got_ref.shape[0]
    state_ref[...] = jnp.zeros_like(state_ref)
    conv_ref[...] = jnp.zeros_like(conv_ref)
    total = jnp.zeros((8, got_ref.shape[2]), F32)
    for r in range(rows):
        slot = carry_ref[r]
        total = total + got_ref[r, 8:16].astype(F32)

        @pl.when(slot >= 0)
        def _():
            state_ref[slot] = got_ref[r, 0:8]
            conv_ref[slot] = got_ref[r, 16:24]

    for i in range(copies_ref.shape[0]):
        copies_ref[i] = total


def final_body(index_ref, got_ref, out_ref):
    rows_own = out_ref.shape[0]
    parts, rows, lanes = got_ref.shape
    flat = got_ref[...].reshape(parts * rows, lanes)
    want = index_ref[0] * rows_own + iota((8, lanes), 0)
    select = jnp.where(iota((8, lanes), 1) == want, 1.0, 0.0)
    out_ref[...] = dot_nt(select, flat, lax.Precision.HIGHEST)[:rows_own]


def exchange(value, axis):
    return lax.all_to_all(value, axis, split_axis=0, concat_axis=0, tiled=True)


def shards(
    tokens_in,
    mix_in,
    step_size,
    doc_ids,
    out_grad,
    proj_weight,
    conv_weight,
    decay_rate,
    carried_state,
    carried_conv,
    carry_from,
):
    _, length, model_width = tokens_in.shape
    slots, heads, part_p, nstate = carried_state.shape
    taps = conv_weight.shape[0]
    parts = lax.axis_size("fsdp")
    tokens = tokens_in[0]
    rows_in = heads * part_p

    flat_conv = carried_conv.reshape(slots, 1, (taps - 1) * rows_in)
    flat_conv = jnp.pad(flat_conv, ((0, 0), (0, 7), (0, nstate - flat_conv.shape[2])))
    stored = jnp.concatenate([carried_state.reshape(slots, rows_in, nstate), flat_conv], axis=1)
    picked = call(pick_body, shaped(stored.shape, BF16), "sv")(carry_from, stored)
    start = exchange(picked, "doc")

    turned = call(turn_body, shaped((parts, 8, proj_weight.shape[0]), BF16), "v")(proj_weight)
    weight = exchange(turned, "fsdp")
    column = call(coeff_body, shaped((parts, 8, length), BF16), "vv")(weight, tokens)
    coeff = exchange(column, "fsdp")

    coeff_part, state_part, conv_part = call(
        row_body,
        (
            shaped((parts, 8, length), BF16),
            shaped((slots, 8, nstate), BF16),
            shaped((slots, 8, nstate), BF16),
        ),
        "svvvvvvv",
        (pltpu.VMEM((length + 8, mix_in.shape[2]), F32), pltpu.VMEM((length + 8, mix_in.shape[2]), F32)),
    )(decay_rate, coeff, mix_in[0], step_size[0], doc_ids, out_grad[0], conv_weight, start)
    coeff_got = exchange(coeff_part, "fsdp")
    back = call(project_body, shaped((slots, 24, nstate), BF16), "vvvv")(
        coeff_got, tokens, state_part, conv_part
    )
    back_got = exchange(back, "doc")
    grad_state, grad_conv, copies = call(
        place_body,
        (
            shaped((slots, 8, nstate), BF16),
            shaped((slots, 8, nstate), BF16),
            shaped((parts, 8, nstate), F32),
        ),
        "sv",
    )(carry_from, back_got)
    got = exchange(copies, "fsdp")
    index = lax.axis_index("fsdp").astype(jnp.int32).reshape(1)
    grad_proj = call(final_body, shaped((model_width // (parts * slots), 2 * nstate), F32), "sv")(
        index, got
    )
    grad_state = grad_state.reshape(carried_state.shape)
    grad_conv = grad_conv[:, 0, : (taps - 1) * rows_in].reshape(carried_conv.shape)
    return (grad_proj, grad_state, grad_conv)


def solution(mesh):
    return jax.shard_map(
        shards,
        mesh=mesh,
        in_specs=(
            P("doc", None, None),
            P("doc", None, "fsdp"),
            P("doc", None, "fsdp"),
            P("doc", None),
            P("doc", None, "fsdp"),
            P("fsdp", None),
            P(None, "fsdp"),
            P("fsdp"),
            P(None, "fsdp", "doc", None),
            P(None, None, "fsdp", "doc"),
            P(),
        ),
        out_specs=(
            P(("doc", "fsdp"), None),
            P(None, "fsdp", "doc", None),
            P(None, None, "fsdp", "doc"),
        ),
        check_vma=False,
    )
```

```python
import functools

import jax
import jax.numpy as jnp
from jax import lax
from jax.experimental import pallas as pl
from jax.experimental.pallas import tpu as pltpu
from jax.sharding import PartitionSpec as P


INTERPRET = False
F32 = jnp.float32
BF16 = jnp.bfloat16


def iota(shape, dim):
    return lax.broadcasted_iota(jnp.int32, shape, dim)


def one_hot(condition):
    return jnp.where(condition, 1.0, 0.0).astype(BF16)


def dot(a, b):
    return jnp.dot(a, b, preferred_element_type=F32)


def dot_nt(a, b, precision=None):
    return lax.dot_general(
        a, b, (((1,), (1,)), ((), ())), precision=precision, preferred_element_type=F32
    )


def halves(value):
    high = value.astype(BF16)
    return high, (value - high.astype(F32)).astype(BF16)


def call(body, out_shape, in_specs, scratch=()):
    vmem = pl.BlockSpec(memory_space=pltpu.VMEM)
    smem = pl.BlockSpec(memory_space=pltpu.SMEM)
    many = isinstance(out_shape, tuple)
    return pl.pallas_call(
        body,
        out_shape=out_shape,
        in_specs=[smem if spec == "s" else vmem for spec in in_specs],
        out_specs=tuple(vmem for _ in out_shape) if many else vmem,
        scratch_shapes=list(scratch),
        interpret=INTERPRET,
    )


def shaped(shape, kind):
    return jax.ShapeDtypeStruct(shape, kind)


def pick_body(carry_ref, slots_ref, picked_ref):
    for r in range(picked_ref.shape[0]):
        source = carry_ref[r]
        row = slots_ref[jnp.maximum(source, 0)]
        picked_ref[r] = jnp.where(source >= 0, row, jnp.zeros_like(row))


def turn_body(weight_ref, turned_ref):
    rows, columns = weight_ref.shape
    turned = weight_ref[...].astype(F32).T
    turned_ref[...] = turned.reshape(columns // 8, 8, rows).astype(BF16)


def coeff_body(weight_ref, tokens_ref, copies_ref):
    parts = weight_ref.shape[0]
    weight = jnp.concatenate([weight_ref[i] for i in range(parts)], axis=1)
    column = dot_nt(weight, tokens_ref[...]).astype(BF16)
    for i in range(parts):
        copies_ref[i] = column


def early_body(
    decay_ref,
    mix_ref,
    step_ref,
    doc_ref,
    grad_ref,
    tap_ref,
    start_ref,
    score_ref,
    scaled_ref,
    carried_ref,
    reach_ref,
    slope_ref,
    ext,
    doc_ext,
):
    length, channels = mix_ref.shape
    heads = step_ref.shape[1]
    head_dim = channels // heads
    taps = tap_ref.shape[0]
    all_rows, nstate = start_ref.shape
    per_doc = slope_ref.shape[1]
    docs = all_rows // per_doc
    part_p = head_dim // docs
    rows_in = heads * part_p
    square = (length, channels)

    start = start_ref[...]
    chan = iota((channels, all_rows), 0)
    place = (
        ((chan % head_dim) // part_p) * per_doc + (chan // head_dim) * part_p + chan % part_p
    )
    state_zero = dot(one_hot(place == iota((channels, all_rows), 1)), start).astype(BF16)
    conv_row = iota((docs, all_rows), 0) * per_doc + rows_in
    conv_in = dot(one_hot(conv_row == iota((docs, all_rows), 1)), start).astype(BF16)
    lane_chan = iota((nstate, channels), 1)
    lane = iota((nstate, channels), 0)
    lane_of = (lane_chan // head_dim) * part_p + lane_chan % part_p
    owner = (iota((docs, channels), 1) % head_dim) // part_p == iota((docs, channels), 0)
    sub = iota((8, channels), 0)
    head_rows = jnp.zeros((8, channels), F32)
    for k in range(taps - 1):
        spread_row = dot(conv_in, one_hot(lane == k * rows_in + lane_of))
        line = jnp.sum(jnp.where(owner, spread_row, 0.0), axis=0, keepdims=True)
        head_rows = jnp.where(sub == 8 - (taps - 1) + k, line, head_rows)

    doc_row = doc_ref[...]
    doc_turned = jnp.broadcast_to(doc_row.astype(F32), (128, length)).T
    doc_col = jnp.concatenate([doc_turned] * (channels // 128), axis=1)
    doc_first = doc_row[0:1, 0:1].astype(F32)
    opening = doc_col == doc_first
    doc_ext[0:8] = jnp.broadcast_to(doc_first, (8, channels))
    doc_ext[8:] = doc_col

    ext[0:8] = head_rows
    ext[8:] = mix_ref[...].astype(F32)
    preact = jnp.zeros(square, F32)
    for k in range(taps):
        same = doc_ext[8 - k : 8 - k + length] == doc_col
        term = tap_ref[k : k + 1] * ext[8 - k : 8 - k + length]
        preact = preact + jnp.where(same, term, 0.0)
    head_of = iota(square, 1) // head_dim
    step = jnp.broadcast_to(step_ref[:, 0:1], square)
    rate = jnp.where(head_of[0:1] == 0, decay_ref[0], 0.0)
    for h in range(1, heads):
        step = jnp.where(head_of == h, step_ref[:, h : h + 1], step)
        rate = jnp.where(head_of[0:1] == h, decay_ref[h], rate)
    gate = 1.0 / (1.0 + jnp.exp(-preact))
    mixed = (preact * gate).astype(BF16).astype(F32)
    values = (step * mixed).astype(BF16)
    g = gate[0:8]
    slope = step[0:8] * g * (1.0 + preact[0:8] * (1.0 - g))
    slope_ref[0, 0:8] = jnp.where(opening[0:8], slope, 0.0)

    time_row = iota((length, length), 0)
    lower = time_row >= iota((length, length), 1)
    lower_one = one_hot(lower)
    change = -(rate * step)
    first = change.astype(BF16)
    second, third = halves(change - first.astype(F32))
    log_decay = dot(lower_one, first) + (dot(lower_one, second) + dot(lower_one, third))
    log_turned = log_decay.T
    allowed = lower & (doc_col == doc_row.astype(F32))
    grad_wide = grad_ref[...].astype(F32)
    score_grad = jnp.zeros((length, length), F32)
    for h in range(heads):
        own = jnp.where(head_of == h, grad_wide, 0.0).astype(BF16)
        products = dot_nt(own, values)
        column = log_decay[:, h * head_dim : h * head_dim + 1]
        spread = column - log_turned[h * head_dim : h * head_dim + 1]
        decays = jnp.where(allowed, jnp.exp(jnp.where(allowed, spread, 0.0)), 0.0)
        score_grad = score_grad + decays * products
    score_high, score_low = halves(score_grad)
    score_ref[0] = score_high
    score_ref[1] = score_low
    edge = jnp.where(opening, jnp.exp(log_decay), 0.0)
    scaled_high, scaled_low = halves(edge * grad_wide)
    scaled_ref[0] = scaled_high
    scaled_ref[1] = scaled_low
    carried_ref[...] = dot(scaled_high, state_zero) + dot(scaled_low, state_zero)

    time = iota(square, 0)
    for s in range(taps - 1):
        inside = (time >= s) & (doc_col == doc_col[s : s + 1])
        spread = jnp.where(inside, log_decay - log_decay[s : s + 1], 0.0)
        reach_ref[s] = jnp.where(inside, jnp.exp(spread) * grad_wide, 0.0).astype(BF16)


def late_body(
    heads,
    coeff_ref,
    score_ref,
    scaled_ref,
    carried_ref,
    reach_ref,
    slope_ref,
    tap_ref,
    coeff_grad_ref,
    state_ref,
    conv_ref,
):
    _, length, channels = scaled_ref.shape
    nstate = carried_ref.shape[1]
    docs, rows_in, _ = state_ref.shape
    taps = tap_ref.shape[0]
    coeff = coeff_ref[...].astype(F32).reshape(2 * nstate, length)
    head_dim = channels // heads
    part_p = head_dim // docs
    write_turned = coeff[:nstate]
    read_turned = coeff[nstate:]
    write = write_turned.T.astype(BF16)
    read_turned = read_turned.astype(BF16)
    score_high = score_ref[0]
    score_low = score_ref[1]
    scaled_high = scaled_ref[0]
    scaled_low = scaled_ref[1]
    read_grad = dot(score_high, write) + dot(score_low, write) + carried_ref[...]
    write_grad = dot(read_turned, score_high) + dot(read_turned, score_low)
    coeff_grad = jnp.concatenate([write_grad, read_grad.T], axis=0)
    coeff_grad_ref[...] = coeff_grad.reshape(coeff_grad_ref.shape).astype(BF16)
    state_grad = dot(read_turned, scaled_high) + dot(read_turned, scaled_low)
    state_grad = state_grad.T.astype(BF16)
    chan = iota((channels, channels), 1)
    place = (
        ((chan % head_dim) // part_p) * rows_in + (chan // head_dim) * part_p + chan % part_p
    )
    to_parts = one_hot(place == iota((channels, channels), 0))
    state_ref[...] = dot(to_parts, state_grad).reshape(state_ref.shape).astype(BF16)

    scores = dot(write[0:16], read_turned)
    score_high, score_low = halves(scores)
    pre_grads = []
    for s in range(taps - 1):
        reach = reach_ref[s]
        value_grad = dot(score_high, reach) + dot(score_low, reach)
        pre_grads.append(value_grad[s : s + 1] * slope_ref[0, s : s + 1])
    lane_chan = iota((nstate, channels), 1)
    lane = iota((nstate, channels), 0)
    lane_of = (lane_chan // head_dim) * part_p + lane_chan % part_p
    owner = (iota((docs, channels), 1) % head_dim) // part_p == iota((docs, channels), 0)
    lines = jnp.zeros((docs, nstate), F32)
    for j in range(taps - 1):
        line = jnp.zeros((1, channels), F32)
        for k in range(taps - 1 - j, taps):
            line = line + tap_ref[k : k + 1] * pre_grads[j - (taps - 1) + k]
        line = jnp.where(owner, jnp.broadcast_to(line, (docs, channels)), 0.0).astype(BF16)
        lines = lines + dot_nt(line, one_hot(lane == j * rows_in + lane_of))
    conv_ref[...] = lines.astype(BF16)


def project_body(got_ref, tokens_ref, out_ref):
    parts = out_ref.shape[0]
    rows = got_ref.shape[1]
    summed = jnp.sum(got_ref[...].astype(F32), axis=0)
    high = summed.astype(BF16).astype(F32)
    both = jnp.concatenate([high, summed - high], axis=0).astype(BF16)
    partial = dot(both, tokens_ref[...])
    partial = (partial[:rows] + partial[rows:]).astype(BF16)
    width = partial.shape[1] // parts
    for d in range(parts):
        out_ref[d] = partial[:, d * width : (d + 1) * width]


def place_body(carry_ref, got_ref, flat_ref, state_ref, conv_ref, copies_ref):
    rows, pairs, _, _ = got_ref.shape
    kept = state_ref.shape[1]
    state_ref[...] = jnp.zeros_like(state_ref)
    conv_ref[...] = jnp.zeros_like(conv_ref)
    for r in range(rows):
        slot = carry_ref[r]

        @pl.when(slot >= 0)
        def _():
            state_ref[slot] = got_ref[r, 0:kept]
            conv_ref[slot] = got_ref[r, pairs - 1 : pairs]

    every = flat_ref.shape[0]
    mine = iota((8, every), 1) % (2 * pairs) == 2 * kept + iota((8, every), 0)
    total = dot(one_hot(mine), flat_ref[...])
    for i in range(copies_ref.shape[0]):
        copies_ref[i] = total


def final_body(index_ref, got_ref, out_ref):
    rows_own = out_ref.shape[0]
    parts, rows, lanes = got_ref.shape
    flat = got_ref[...].reshape(parts * rows, lanes)
    want = index_ref[0] * rows_own + iota((8, lanes), 0)
    select = jnp.where(iota((8, lanes), 1) == want, 1.0, 0.0)
    out_ref[...] = dot_nt(select, flat, lax.Precision.HIGHEST)[:rows_own]


def exchange(value, axis):
    return lax.all_to_all(value, axis, split_axis=0, concat_axis=0, tiled=True)


def shards(
    tokens_in,
    mix_in,
    step_size,
    doc_ids,
    out_grad,
    proj_weight,
    conv_weight,
    decay_rate,
    carried_state,
    carried_conv,
    carry_from,
):
    _, length, model_width = tokens_in.shape
    slots, heads, part_p, nstate = carried_state.shape
    taps = conv_weight.shape[0]
    parts = lax.axis_size("fsdp")
    tokens = tokens_in[0]
    rows_in = heads * part_p

    flat_conv = carried_conv.reshape(slots, 1, 1, (taps - 1) * rows_in)
    flat_conv = jnp.pad(flat_conv, ((0, 0), (0, 0), (0, 1), (0, nstate - flat_conv.shape[3])))
    stored = carried_state.reshape(slots, rows_in // 2, 2, nstate)
    stored = jnp.concatenate([stored, flat_conv], axis=1)
    picked = call(pick_body, shaped(stored.shape, BF16), "sv")(carry_from, stored)
    start = exchange(picked, "doc").reshape(slots * (rows_in + 2), nstate)

    turned = call(turn_body, shaped((parts, 8, proj_weight.shape[0]), BF16), "v")(proj_weight)
    weight = exchange(turned, "fsdp")
    column = call(coeff_body, shaped((parts, 8, length), BF16), "vv")(weight, tokens)
    coeff = exchange(column, "fsdp")

    channels = mix_in.shape[2]
    kept = call(
        early_body,
        (
            shaped((2, length, length), BF16),
            shaped((2, length, channels), BF16),
            shaped((length, nstate), F32),
            shaped((taps - 1, length, channels), BF16),
            shaped((1, rows_in + 2, channels), F32),
        ),
        "svvvvvv",
        (pltpu.VMEM((length + 8, channels), F32), pltpu.VMEM((length + 8, channels), F32)),
    )(decay_rate, mix_in[0], step_size[0], doc_ids, out_grad[0], conv_weight, start)
    coeff_part, state_part, conv_part = call(
        functools.partial(late_body, heads),
        (
            shaped((parts, 8, length), BF16),
            shaped((slots, rows_in, nstate), BF16),
            shaped((slots, nstate), BF16),
        ),
        "vvvvvvv",
    )(coeff, *kept, conv_weight)
    coeff_got = exchange(coeff_part, "fsdp")
    share = call(project_body, shaped((slots, 8, nstate), BF16), "vv")(coeff_got, tokens)
    conv_part = jnp.pad(conv_part.reshape(slots, 1, 1, nstate), ((0, 0), (0, 0), (0, 1), (0, 0)))
    back = jnp.concatenate(
        [
            state_part.reshape(slots, rows_in // 2, 2, nstate),
            share.reshape(slots, 4, 2, nstate),
            conv_part,
        ],
        axis=1,
    )
    back_got = exchange(back, "doc")
    grad_state, grad_conv, copies = call(
        place_body,
        (
            shaped((slots, rows_in // 2, 2, nstate), BF16),
            shaped((slots, 1, 2, nstate), BF16),
            shaped((parts, 8, nstate), F32),
        ),
        "svv",
    )(carry_from, back_got, back_got.reshape(-1, nstate))
    got = exchange(copies, "fsdp")
    index = lax.axis_index("fsdp").astype(jnp.int32).reshape(1)
    grad_proj = call(
        final_body, shaped((model_width // (parts * slots), 2 * nstate), F32), "sv"
    )(index, got)
    grad_state = grad_state.reshape(carried_state.shape)
    grad_conv = grad_conv[:, 0, 0, : (taps - 1) * rows_in].reshape(carried_conv.shape)
    return (grad_proj, grad_state, grad_conv)


def solution(mesh):
    return jax.shard_map(
        shards,
        mesh=mesh,
        in_specs=(
            P("doc", None, None),
            P("doc", None, "fsdp"),
            P("doc", None, "fsdp"),
            P("doc", None),
            P("doc", None, "fsdp"),
            P("fsdp", None),
            P(None, "fsdp"),
            P("fsdp"),
            P(None, "fsdp", "doc", None),
            P(None, None, "fsdp", "doc"),
            P(),
        ),
        out_specs=(
            P(("doc", "fsdp"), None),
            P(None, "fsdp", "doc", None),
            P(None, None, "fsdp", "doc"),
        ),
        check_vma=False,
    )
```

```python
import functools

import jax
import jax.numpy as jnp
from jax import lax
from jax.experimental import pallas as pl
from jax.experimental.pallas import tpu as pltpu
from jax.sharding import PartitionSpec as P


INTERPRET = False
LIMIT = 24 * 1024 * 1024
F32 = jnp.float32
BF16 = jnp.bfloat16


def iota(shape, dim):
    return lax.broadcasted_iota(jnp.int32, shape, dim)


def one_hot(condition):
    return jnp.where(condition, 1.0, 0.0).astype(BF16)


def dot(a, b):
    return jnp.dot(a, b, preferred_element_type=F32)


def dot_nt(a, b, precision=None):
    return lax.dot_general(
        a, b, (((1,), (1,)), ((), ())), precision=precision, preferred_element_type=F32
    )


def halves(value):
    high = value.astype(BF16)
    return high, (value - high.astype(F32)).astype(BF16)


def call(body, out_shape, in_specs, scratch=()):
    vmem = pl.BlockSpec(memory_space=pltpu.VMEM)
    smem = pl.BlockSpec(memory_space=pltpu.SMEM)
    many = isinstance(out_shape, tuple)
    return pl.pallas_call(
        body,
        out_shape=out_shape,
        in_specs=[smem if spec == "s" else vmem for spec in in_specs],
        out_specs=tuple(vmem for _ in out_shape) if many else vmem,
        scratch_shapes=list(scratch),
        compiler_params=pltpu.CompilerParams(vmem_limit_bytes=LIMIT),
        interpret=INTERPRET,
    )


def shaped(shape, kind):
    return jax.ShapeDtypeStruct(shape, kind)


def pick_body(carry_ref, slots_ref, picked_ref):
    for r in range(picked_ref.shape[0]):
        source = carry_ref[r]
        row = slots_ref[jnp.maximum(source, 0)]
        picked_ref[r] = jnp.where(source >= 0, row, jnp.zeros_like(row))


def turn_body(weight_ref, turned_ref):
    rows, columns = weight_ref.shape
    turned = weight_ref[...].astype(F32).T
    turned_ref[...] = turned.reshape(columns // 8, 8, rows).astype(BF16)


def coeff_body(weight_ref, tokens_ref, copies_ref):
    parts = weight_ref.shape[0]
    weight = jnp.concatenate([weight_ref[i] for i in range(parts)], axis=1)
    column = dot_nt(weight, tokens_ref[...]).astype(BF16)
    for i in range(parts):
        copies_ref[i] = column


def early_body(
    decay_ref,
    mix_ref,
    step_ref,
    doc_ref,
    grad_ref,
    tap_ref,
    start_ref,
    score_ref,
    scaled_ref,
    carried_ref,
    reach_ref,
    slope_ref,
    ext,
    doc_ext,
):
    length, channels = mix_ref.shape
    heads = step_ref.shape[1]
    head_dim = channels // heads
    taps = tap_ref.shape[0]
    all_rows, nstate = start_ref.shape
    per_doc = slope_ref.shape[1]
    docs = all_rows // per_doc
    part_p = head_dim // docs
    rows_in = heads * part_p
    square = (length, channels)

    start = start_ref[...]
    chan = iota((channels, all_rows), 0)
    place = (
        ((chan % head_dim) // part_p) * per_doc + (chan // head_dim) * part_p + chan % part_p
    )
    state_zero = dot(one_hot(place == iota((channels, all_rows), 1)), start).astype(BF16)
    conv_row = iota((docs, all_rows), 0) * per_doc + rows_in
    conv_in = dot(one_hot(conv_row == iota((docs, all_rows), 1)), start).astype(BF16)
    lane_chan = iota((nstate, channels), 1)
    lane = iota((nstate, channels), 0)
    lane_of = (lane_chan // head_dim) * part_p + lane_chan % part_p
    owner = (iota((docs, channels), 1) % head_dim) // part_p == iota((docs, channels), 0)
    sub = iota((8, channels), 0)
    head_rows = jnp.zeros((8, channels), F32)
    for k in range(taps - 1):
        spread_row = dot(conv_in, one_hot(lane == k * rows_in + lane_of))
        line = jnp.sum(jnp.where(owner, spread_row, 0.0), axis=0, keepdims=True)
        head_rows = jnp.where(sub == 8 - (taps - 1) + k, line, head_rows)

    doc_row = doc_ref[...]
    doc_turned = jnp.broadcast_to(doc_row.astype(F32), (128, length)).T
    doc_col = jnp.concatenate([doc_turned] * (channels // 128), axis=1)
    doc_first = doc_row[0:1, 0:1].astype(F32)
    opening = doc_col == doc_first
    doc_ext[0:8] = jnp.broadcast_to(doc_first, (8, channels))
    doc_ext[8:] = doc_col

    ext[0:8] = head_rows
    ext[8:] = mix_ref[...].astype(F32)
    preact = jnp.zeros(square, F32)
    for k in range(taps):
        same = doc_ext[8 - k : 8 - k + length] == doc_col
        term = tap_ref[k : k + 1] * ext[8 - k : 8 - k + length]
        preact = preact + jnp.where(same, term, 0.0)
    head_of = iota(square, 1) // head_dim
    step = jnp.broadcast_to(step_ref[:, 0:1], square)
    rate = jnp.where(head_of[0:1] == 0, decay_ref[0], 0.0)
    for h in range(1, heads):
        step = jnp.where(head_of == h, step_ref[:, h : h + 1], step)
        rate = jnp.where(head_of[0:1] == h, decay_ref[h], rate)
    gate = 1.0 / (1.0 + jnp.exp(-preact))
    mixed = (preact * gate).astype(BF16).astype(F32)
    values = (step * mixed).astype(BF16)
    g = gate[0:8]
    slope = step[0:8] * g * (1.0 + preact[0:8] * (1.0 - g))
    slope_ref[0, 0:8] = jnp.where(opening[0:8], slope, 0.0)

    time_row = iota((length, length), 0)
    lower = time_row >= iota((length, length), 1)
    lower_one = one_hot(lower)
    change = -(rate * step)
    first = change.astype(BF16)
    second, third = halves(change - first.astype(F32))
    log_decay = dot(lower_one, first) + (dot(lower_one, second) + dot(lower_one, third))
    log_turned = log_decay.T
    allowed = lower & (doc_col == doc_row.astype(F32))
    grad_wide = grad_ref[...].astype(F32)
    score_grad = jnp.zeros((length, length), F32)
    for h in range(heads):
        own = jnp.where(head_of == h, grad_wide, 0.0).astype(BF16)
        products = dot_nt(own, values)
        column = log_decay[:, h * head_dim : h * head_dim + 1]
        spread = column - log_turned[h * head_dim : h * head_dim + 1]
        decays = jnp.where(allowed, jnp.exp(jnp.where(allowed, spread, 0.0)), 0.0)
        score_grad = score_grad + decays * products
    score_high, score_low = halves(score_grad)
    score_ref[0] = score_high
    score_ref[1] = score_low
    edge = jnp.where(opening, jnp.exp(log_decay), 0.0)
    scaled_high, scaled_low = halves(edge * grad_wide)
    scaled_ref[0] = scaled_high
    scaled_ref[1] = scaled_low
    carried_ref[...] = dot(scaled_high, state_zero) + dot(scaled_low, state_zero)

    time = iota(square, 0)
    for s in range(taps - 1):
        inside = (time >= s) & (doc_col == doc_col[s : s + 1])
        spread = jnp.where(inside, log_decay - log_decay[s : s + 1], 0.0)
        reach_ref[s] = jnp.where(inside, jnp.exp(spread) * grad_wide, 0.0).astype(BF16)


def columns_body(coeff_ref, score_ref, carried_ref, coeff_grad_ref):
    length, nstate = carried_ref.shape
    coeff = coeff_ref[...].astype(F32).reshape(2 * nstate, length)
    write = coeff[:nstate].T.astype(BF16)
    read_turned = coeff[nstate:].astype(BF16)
    score_high = score_ref[0]
    score_low = score_ref[1]
    read_grad = dot(score_high, write) + dot(score_low, write) + carried_ref[...]
    write_grad = dot(read_turned, score_high) + dot(read_turned, score_low)
    coeff_grad = jnp.concatenate([write_grad, read_grad.T], axis=0)
    coeff_grad_ref[...] = coeff_grad.reshape(coeff_grad_ref.shape).astype(BF16)


def state_body(heads, coeff_ref, scaled_ref, reach_ref, slope_ref, tap_ref, state_ref, conv_ref):
    _, length, channels = scaled_ref.shape
    docs, rows_in, nstate = state_ref.shape
    taps = tap_ref.shape[0]
    coeff = coeff_ref[...].astype(F32).reshape(2 * nstate, length)
    head_dim = channels // heads
    part_p = head_dim // docs
    write = coeff[:nstate].T.astype(BF16)
    read_turned = coeff[nstate:].astype(BF16)
    state_grad = dot(read_turned, scaled_ref[0]) + dot(read_turned, scaled_ref[1])
    state_grad = state_grad.T.astype(BF16)
    chan = iota((channels, channels), 1)
    place = (
        ((chan % head_dim) // part_p) * rows_in + (chan // head_dim) * part_p + chan % part_p
    )
    to_parts = one_hot(place == iota((channels, channels), 0))
    state_ref[...] = dot(to_parts, state_grad).reshape(state_ref.shape).astype(BF16)

    scores = dot(write[0:16], read_turned)
    score_high, score_low = halves(scores)
    pre_grads = []
    for s in range(taps - 1):
        reach = reach_ref[s]
        value_grad = dot(score_high, reach) + dot(score_low, reach)
        pre_grads.append(value_grad[s : s + 1] * slope_ref[0, s : s + 1])
    lane_chan = iota((nstate, channels), 1)
    lane = iota((nstate, channels), 0)
    lane_of = (lane_chan // head_dim) * part_p + lane_chan % part_p
    owner = (iota((docs, channels), 1) % head_dim) // part_p == iota((docs, channels), 0)
    lines = jnp.zeros((docs, nstate), F32)
    for j in range(taps - 1):
        line = jnp.zeros((1, channels), F32)
        for k in range(taps - 1 - j, taps):
            line = line + tap_ref[k : k + 1] * pre_grads[j - (taps - 1) + k]
        line = jnp.where(owner, jnp.broadcast_to(line, (docs, channels)), 0.0).astype(BF16)
        lines = lines + dot_nt(line, one_hot(lane == j * rows_in + lane_of))
    conv_ref[...] = lines.astype(BF16)


def project_body(got_ref, tokens_ref, state_ref, conv_ref, out_ref):
    parts = out_ref.shape[0]
    kept = state_ref.shape[1]
    rows = got_ref.shape[1]
    summed = jnp.sum(got_ref[...].astype(F32), axis=0)
    high = summed.astype(BF16).astype(F32)
    both = jnp.concatenate([high, summed - high], axis=0).astype(BF16)
    partial = dot(both, tokens_ref[...])
    partial = partial[:rows] + partial[rows:]
    width = partial.shape[1] // parts
    out_ref[:, 0:kept] = state_ref[...]
    out_ref[:, kept + rows // 2 :] = conv_ref[...]
    for d in range(parts):
        block = partial[:, d * width : (d + 1) * width]
        for k in range(rows // 2):
            out_ref[d, kept + k] = block[2 * k : 2 * k + 2].astype(BF16)


def total_body(pairs, kept, flat_ref, copies_ref):
    every = flat_ref.shape[0]
    mine = iota((8, every), 1) % (2 * pairs) == 2 * kept + iota((8, every), 0)
    total = dot(one_hot(mine), flat_ref[...])
    for i in range(copies_ref.shape[0]):
        copies_ref[i] = total


def place_body(carry_ref, got_ref, state_ref, conv_ref):
    rows, pairs, _, _ = got_ref.shape
    kept = state_ref.shape[1]
    state_ref[...] = jnp.zeros_like(state_ref)
    conv_ref[...] = jnp.zeros_like(conv_ref)
    for r in range(rows):
        slot = carry_ref[r]

        @pl.when(slot >= 0)
        def _():
            state_ref[slot] = got_ref[r, 0:kept]
            conv_ref[slot] = got_ref[r, pairs - 1 : pairs]


def final_body(index_ref, got_ref, out_ref):
    rows_own = out_ref.shape[0]
    parts, rows, lanes = got_ref.shape
    flat = got_ref[...].reshape(parts * rows, lanes)
    want = index_ref[0] * rows_own + iota((8, lanes), 0)
    select = jnp.where(iota((8, lanes), 1) == want, 1.0, 0.0)
    out_ref[...] = dot_nt(select, flat, lax.Precision.HIGHEST)[:rows_own]


def exchange(value, axis):
    return lax.all_to_all(value, axis, split_axis=0, concat_axis=0, tiled=True)


def shards(
    tokens_in,
    mix_in,
    step_size,
    doc_ids,
    out_grad,
    proj_weight,
    conv_weight,
    decay_rate,
    carried_state,
    carried_conv,
    carry_from,
):
    _, length, model_width = tokens_in.shape
    slots, heads, part_p, nstate = carried_state.shape
    taps = conv_weight.shape[0]
    parts = lax.axis_size("fsdp")
    tokens = tokens_in[0]
    rows_in = heads * part_p

    flat_conv = carried_conv.reshape(slots, 1, 1, (taps - 1) * rows_in)
    flat_conv = jnp.pad(flat_conv, ((0, 0), (0, 0), (0, 1), (0, nstate - flat_conv.shape[3])))
    stored = carried_state.reshape(slots, rows_in // 2, 2, nstate)
    stored = jnp.concatenate([stored, flat_conv], axis=1)
    picked = call(pick_body, shaped(stored.shape, BF16), "sv")(carry_from, stored)
    start = exchange(picked, "doc").reshape(slots * (rows_in + 2), nstate)

    turned = call(turn_body, shaped((parts, 8, proj_weight.shape[0]), BF16), "v")(proj_weight)
    weight = exchange(turned, "fsdp")
    column = call(coeff_body, shaped((parts, 8, length), BF16), "vv")(weight, tokens)
    coeff = exchange(column, "fsdp")

    channels = mix_in.shape[2]
    kept = call(
        early_body,
        (
            shaped((2, length, length), BF16),
            shaped((2, length, channels), BF16),
            shaped((length, nstate), F32),
            shaped((taps - 1, length, channels), BF16),
            shaped((1, rows_in + 2, channels), F32),
        ),
        "svvvvvv",
        (pltpu.VMEM((length + 8, channels), F32), pltpu.VMEM((length + 8, channels), F32)),
    )(decay_rate, mix_in[0], step_size[0], doc_ids, out_grad[0], conv_weight, start)
    scores, scaled, carried, reach, slope = kept
    coeff_part = call(columns_body, shaped((parts, 8, length), BF16), "vvv")(coeff, scores, carried)
    coeff_got = exchange(coeff_part, "fsdp")
    state_part, conv_part = call(
        functools.partial(state_body, heads),
        (shaped((slots, rows_in, nstate), BF16), shaped((slots, nstate), BF16)),
        "vvvvv",
    )(coeff, scaled, reach, slope, conv_weight)
    state_pairs = rows_in // 2
    conv_part = jnp.pad(conv_part.reshape(slots, 1, 1, nstate), ((0, 0), (0, 0), (0, 1), (0, 0)))
    pairs = state_pairs + 5
    back = call(project_body, shaped((slots, pairs, 2, nstate), BF16), "vvvv")(
        coeff_got, tokens, state_part.reshape(slots, state_pairs, 2, nstate), conv_part
    )
    back_got = exchange(back, "doc")
    copies = call(
        functools.partial(total_body, pairs, state_pairs), shaped((parts, 8, nstate), F32), "v"
    )(back_got.reshape(-1, nstate))
    got = exchange(copies, "fsdp")
    grad_state, grad_conv = call(
        place_body,
        (shaped((slots, state_pairs, 2, nstate), BF16), shaped((slots, 1, 2, nstate), BF16)),
        "sv",
    )(carry_from, back_got)
    index = lax.axis_index("fsdp").astype(jnp.int32).reshape(1)
    grad_proj = call(
        final_body, shaped((model_width // (parts * slots), 2 * nstate), F32), "sv"
    )(index, got)
    grad_state = grad_state.reshape(carried_state.shape)
    grad_conv = grad_conv[:, 0, 0, : (taps - 1) * rows_in].reshape(carried_conv.shape)
    return (grad_proj, grad_state, grad_conv)


def solution(mesh):
    return jax.shard_map(
        shards,
        mesh=mesh,
        in_specs=(
            P("doc", None, None),
            P("doc", None, "fsdp"),
            P("doc", None, "fsdp"),
            P("doc", None),
            P("doc", None, "fsdp"),
            P("fsdp", None),
            P(None, "fsdp"),
            P("fsdp"),
            P(None, "fsdp", "doc", None),
            P(None, None, "fsdp", "doc"),
            P(),
        ),
        out_specs=(
            P(("doc", "fsdp"), None),
            P(None, "fsdp", "doc", None),
            P(None, None, "fsdp", "doc"),
        ),
        check_vma=False,
    )
```

```python
import functools

import jax
import jax.numpy as jnp
from jax import lax
from jax.experimental import pallas as pl
from jax.experimental.pallas import tpu as pltpu
from jax.sharding import PartitionSpec as P


INTERPRET = False
LIMIT = 24 * 1024 * 1024
F32 = jnp.float32
BF16 = jnp.bfloat16


def iota(shape, dim):
    return lax.broadcasted_iota(jnp.int32, shape, dim)


def one_hot(condition):
    return jnp.where(condition, 1.0, 0.0).astype(BF16)


def dot(a, b):
    return jnp.dot(a, b, preferred_element_type=F32)


def dot_nt(a, b, precision=None):
    return lax.dot_general(
        a, b, (((1,), (1,)), ((), ())), precision=precision, preferred_element_type=F32
    )


def halves(value):
    high = value.astype(BF16)
    return high, (value - high.astype(F32)).astype(BF16)


def call(body, out_shape, in_specs, scratch=()):
    vmem = pl.BlockSpec(memory_space=pltpu.VMEM)
    smem = pl.BlockSpec(memory_space=pltpu.SMEM)
    many = isinstance(out_shape, tuple)
    return pl.pallas_call(
        body,
        out_shape=out_shape,
        in_specs=[smem if spec == "s" else vmem for spec in in_specs],
        out_specs=tuple(vmem for _ in out_shape) if many else vmem,
        scratch_shapes=list(scratch),
        compiler_params=pltpu.CompilerParams(vmem_limit_bytes=LIMIT),
        interpret=INTERPRET,
    )


def shaped(shape, kind):
    return jax.ShapeDtypeStruct(shape, kind)


def pick_body(carry_ref, slots_ref, picked_ref):
    for r in range(picked_ref.shape[0]):
        source = carry_ref[r]
        row = slots_ref[jnp.maximum(source, 0)]
        picked_ref[r] = jnp.where(source >= 0, row, jnp.zeros_like(row))


def turn_body(weight_ref, turned_ref):
    rows, columns = weight_ref.shape
    turned = weight_ref[...].astype(F32).T
    turned_ref[...] = turned.reshape(columns // 8, 8, rows).astype(BF16)


def coeff_body(weight_ref, tokens_ref, copies_ref):
    parts = weight_ref.shape[0]
    weight = jnp.concatenate([weight_ref[i] for i in range(parts)], axis=1)
    column = dot_nt(weight, tokens_ref[...]).astype(BF16)
    for i in range(parts):
        copies_ref[i] = column


def early_body(
    decay_ref,
    mix_ref,
    step_ref,
    doc_ref,
    grad_ref,
    tap_ref,
    start_ref,
    score_ref,
    scaled_ref,
    carried_ref,
    reach_ref,
    slope_ref,
    ext,
    doc_ext,
):
    length, channels = mix_ref.shape
    heads = step_ref.shape[1]
    head_dim = channels // heads
    taps = tap_ref.shape[0]
    all_rows, nstate = start_ref.shape
    per_doc = slope_ref.shape[1]
    docs = all_rows // per_doc
    part_p = head_dim // docs
    rows_in = heads * part_p
    square = (length, channels)

    start = start_ref[...]
    chan = iota((channels, all_rows), 0)
    place = (
        ((chan % head_dim) // part_p) * per_doc + (chan // head_dim) * part_p + chan % part_p
    )
    state_zero = dot(one_hot(place == iota((channels, all_rows), 1)), start).astype(BF16)
    conv_row = iota((docs, all_rows), 0) * per_doc + rows_in
    conv_in = dot(one_hot(conv_row == iota((docs, all_rows), 1)), start).astype(BF16)
    lane_chan = iota((nstate, channels), 1)
    lane = iota((nstate, channels), 0)
    lane_of = (lane_chan // head_dim) * part_p + lane_chan % part_p
    owner = (iota((docs, channels), 1) % head_dim) // part_p == iota((docs, channels), 0)
    sub = iota((8, channels), 0)
    head_rows = jnp.zeros((8, channels), F32)
    for k in range(taps - 1):
        spread_row = dot(conv_in, one_hot(lane == k * rows_in + lane_of))
        line = jnp.sum(jnp.where(owner, spread_row, 0.0), axis=0, keepdims=True)
        head_rows = jnp.where(sub == 8 - (taps - 1) + k, line, head_rows)

    doc_row = doc_ref[...]
    doc_turned = jnp.broadcast_to(doc_row.astype(F32), (128, length)).T
    doc_col = jnp.concatenate([doc_turned] * (channels // 128), axis=1)
    doc_first = doc_row[0:1, 0:1].astype(F32)
    opening = doc_col == doc_first
    doc_ext[0:8] = jnp.broadcast_to(doc_first, (8, channels))
    doc_ext[8:] = doc_col

    ext[0:8] = head_rows
    ext[8:] = mix_ref[...].astype(F32)
    preact = jnp.zeros(square, F32)
    for k in range(taps):
        same = doc_ext[8 - k : 8 - k + length] == doc_col
        term = tap_ref[k : k + 1] * ext[8 - k : 8 - k + length]
        preact = preact + jnp.where(same, term, 0.0)
    head_of = iota(square, 1) // head_dim
    step = jnp.broadcast_to(step_ref[:, 0:1], square)
    rate = jnp.where(head_of[0:1] == 0, decay_ref[0], 0.0)
    for h in range(1, heads):
        step = jnp.where(head_of == h, step_ref[:, h : h + 1], step)
        rate = jnp.where(head_of[0:1] == h, decay_ref[h], rate)
    gate = 1.0 / (1.0 + jnp.exp(-preact))
    mixed = (preact * gate).astype(BF16).astype(F32)
    values = (step * mixed).astype(BF16)
    g = gate[0:8]
    slope = step[0:8] * g * (1.0 + preact[0:8] * (1.0 - g))
    slope_ref[0, 0:8] = jnp.where(opening[0:8], slope, 0.0)

    time_row = iota((length, length), 0)
    lower = time_row >= iota((length, length), 1)
    lower_one = one_hot(lower)
    change = -(rate * step)
    first = change.astype(BF16)
    second, third = halves(change - first.astype(F32))
    log_decay = dot(lower_one, first) + (dot(lower_one, second) + dot(lower_one, third))
    log_turned = log_decay.T
    allowed = lower & (doc_col == doc_row.astype(F32))
    grad_wide = grad_ref[...].astype(F32)
    score_grad = jnp.zeros((length, length), F32)
    for h in range(heads):
        own = jnp.where(head_of == h, grad_wide, 0.0).astype(BF16)
        products = dot_nt(own, values)
        column = log_decay[:, h * head_dim : h * head_dim + 1]
        spread = column - log_turned[h * head_dim : h * head_dim + 1]
        decays = jnp.where(allowed, jnp.exp(jnp.where(allowed, spread, 0.0)), 0.0)
        score_grad = score_grad + decays * products
    score_high, score_low = halves(score_grad)
    score_ref[0] = score_high
    score_ref[1] = score_low
    edge = jnp.where(opening, jnp.exp(log_decay), 0.0)
    scaled_high, scaled_low = halves(edge * grad_wide)
    scaled_ref[...] = scaled_high
    carried = dot(scaled_high, state_zero) + dot(scaled_low, state_zero)
    carried_high, carried_low = halves(carried.T)
    carried_ref[0] = carried_high
    carried_ref[1] = carried_low

    time = iota(square, 0)
    for s in range(taps - 1):
        inside = (time >= s) & (doc_col == doc_col[s : s + 1])
        spread = jnp.where(inside, log_decay - log_decay[s : s + 1], 0.0)
        reach_ref[s] = jnp.where(inside, jnp.exp(spread) * grad_wide, 0.0).astype(BF16)


def columns_body(coeff_ref, score_ref, carried_ref, coeff_grad_ref):
    _, nstate, length = carried_ref.shape
    coeff = coeff_ref[...].astype(F32).reshape(2 * nstate, length)
    write_turned = coeff[:nstate].astype(BF16)
    read_turned = coeff[nstate:].astype(BF16)
    score_high = score_ref[0]
    score_low = score_ref[1]
    read_grad = dot_nt(write_turned, score_high) + dot_nt(write_turned, score_low)
    read_grad = read_grad + (carried_ref[0].astype(F32) + carried_ref[1].astype(F32))
    write_grad = dot(read_turned, score_high) + dot(read_turned, score_low)
    coeff_grad = jnp.concatenate([write_grad, read_grad], axis=0)
    coeff_grad_ref[...] = coeff_grad.reshape(coeff_grad_ref.shape).astype(BF16)


def state_body(heads, coeff_ref, scaled_ref, reach_ref, slope_ref, tap_ref, state_ref, conv_ref):
    length, channels = scaled_ref.shape
    docs, rows_in, nstate = state_ref.shape
    taps = tap_ref.shape[0]
    coeff = coeff_ref[...].astype(F32).reshape(2 * nstate, length)
    head_dim = channels // heads
    part_p = head_dim // docs
    write = coeff[:nstate].T.astype(BF16)
    read_turned = coeff[nstate:].astype(BF16)
    state_grad = dot(read_turned, scaled_ref[...])
    state_grad = state_grad.T.astype(BF16)
    chan = iota((channels, channels), 1)
    place = (
        ((chan % head_dim) // part_p) * rows_in + (chan // head_dim) * part_p + chan % part_p
    )
    to_parts = one_hot(place == iota((channels, channels), 0))
    state_ref[...] = dot(to_parts, state_grad).reshape(state_ref.shape).astype(BF16)

    scores = dot(write[0:16], read_turned)
    score_high, score_low = halves(scores)
    pre_grads = []
    for s in range(taps - 1):
        reach = reach_ref[s]
        value_grad = dot(score_high, reach) + dot(score_low, reach)
        pre_grads.append(value_grad[s : s + 1] * slope_ref[0, s : s + 1])
    lane_chan = iota((nstate, channels), 1)
    lane = iota((nstate, channels), 0)
    lane_of = (lane_chan // head_dim) * part_p + lane_chan % part_p
    owner = (iota((docs, channels), 1) % head_dim) // part_p == iota((docs, channels), 0)
    lines = jnp.zeros((docs, nstate), F32)
    for j in range(taps - 1):
        line = jnp.zeros((1, channels), F32)
        for k in range(taps - 1 - j, taps):
            line = line + tap_ref[k : k + 1] * pre_grads[j - (taps - 1) + k]
        line = jnp.where(owner, jnp.broadcast_to(line, (docs, channels)), 0.0).astype(BF16)
        lines = lines + dot_nt(line, one_hot(lane == j * rows_in + lane_of))
    conv_ref[...] = lines.astype(BF16)


def project_body(got_ref, tokens_ref, state_ref, conv_ref, out_ref):
    parts = out_ref.shape[0]
    kept = state_ref.shape[1]
    rows = got_ref.shape[1]
    summed = jnp.sum(got_ref[...].astype(F32), axis=0)
    high = summed.astype(BF16).astype(F32)
    both = jnp.concatenate([high, summed - high], axis=0).astype(BF16)
    partial = dot(both, tokens_ref[...])
    partial = partial[:rows] + partial[rows:]
    width = partial.shape[1] // parts
    out_ref[:, 0:kept] = state_ref[...]
    out_ref[:, kept + rows // 2 :] = conv_ref[...]
    for d in range(parts):
        block = partial[:, d * width : (d + 1) * width]
        for k in range(rows // 2):
            out_ref[d, kept + k] = block[2 * k : 2 * k + 2].astype(BF16)


def total_body(pairs, kept, flat_ref, copies_ref):
    every = flat_ref.shape[0]
    mine = iota((8, every), 1) % (2 * pairs) == 2 * kept + iota((8, every), 0)
    total = dot(one_hot(mine), flat_ref[...])
    for i in range(copies_ref.shape[0]):
        copies_ref[i] = total


def place_body(carry_ref, got_ref, state_ref, conv_ref):
    rows, pairs, _, _ = got_ref.shape
    kept = state_ref.shape[1]
    state_ref[...] = jnp.zeros_like(state_ref)
    conv_ref[...] = jnp.zeros_like(conv_ref)
    for r in range(rows):
        slot = carry_ref[r]

        @pl.when(slot >= 0)
        def _():
            state_ref[slot] = got_ref[r, 0:kept]
            conv_ref[slot] = got_ref[r, pairs - 1 : pairs]


def final_body(index_ref, got_ref, out_ref):
    rows_own = out_ref.shape[0]
    parts, rows, lanes = got_ref.shape
    flat = got_ref[...].reshape(parts * rows, lanes)
    want = index_ref[0] * rows_own + iota((8, lanes), 0)
    select = jnp.where(iota((8, lanes), 1) == want, 1.0, 0.0)
    out_ref[...] = dot_nt(select, flat, lax.Precision.HIGHEST)[:rows_own]


def exchange(value, axis):
    return lax.all_to_all(value, axis, split_axis=0, concat_axis=0, tiled=True)


def shards(
    tokens_in,
    mix_in,
    step_size,
    doc_ids,
    out_grad,
    proj_weight,
    conv_weight,
    decay_rate,
    carried_state,
    carried_conv,
    carry_from,
):
    _, length, model_width = tokens_in.shape
    slots, heads, part_p, nstate = carried_state.shape
    taps = conv_weight.shape[0]
    parts = lax.axis_size("fsdp")
    tokens = tokens_in[0]
    rows_in = heads * part_p

    flat_conv = carried_conv.reshape(slots, 1, 1, (taps - 1) * rows_in)
    flat_conv = jnp.pad(flat_conv, ((0, 0), (0, 0), (0, 1), (0, nstate - flat_conv.shape[3])))
    stored = carried_state.reshape(slots, rows_in // 2, 2, nstate)
    stored = jnp.concatenate([stored, flat_conv], axis=1)
    picked = call(pick_body, shaped(stored.shape, BF16), "sv")(carry_from, stored)
    start = exchange(picked, "doc").reshape(slots * (rows_in + 2), nstate)

    turned = call(turn_body, shaped((parts, 8, proj_weight.shape[0]), BF16), "v")(proj_weight)
    weight = exchange(turned, "fsdp")
    column = call(coeff_body, shaped((parts, 8, length), BF16), "vv")(weight, tokens)
    coeff = exchange(column, "fsdp")

    channels = mix_in.shape[2]
    kept = call(
        early_body,
        (
            shaped((2, length, length), BF16),
            shaped((length, channels), BF16),
            shaped((2, nstate, length), BF16),
            shaped((taps - 1, length, channels), BF16),
            shaped((1, rows_in + 2, channels), F32),
        ),
        "svvvvvv",
        (pltpu.VMEM((length + 8, channels), F32), pltpu.VMEM((length + 8, channels), F32)),
    )(decay_rate, mix_in[0], step_size[0], doc_ids, out_grad[0], conv_weight, start)
    scores, scaled, carried, reach, slope = kept
    coeff_part = call(columns_body, shaped((parts, 8, length), BF16), "vvv")(coeff, scores, carried)
    coeff_got = exchange(coeff_part, "fsdp")
    state_part, conv_part = call(
        functools.partial(state_body, heads),
        (shaped((slots, rows_in, nstate), BF16), shaped((slots, nstate), BF16)),
        "vvvvv",
    )(coeff, scaled, reach, slope, conv_weight)
    state_pairs = rows_in // 2
    conv_part = jnp.pad(conv_part.reshape(slots, 1, 1, nstate), ((0, 0), (0, 0), (0, 1), (0, 0)))
    pairs = state_pairs + 5
    back = call(project_body, shaped((slots, pairs, 2, nstate), BF16), "vvvv")(
        coeff_got, tokens, state_part.reshape(slots, state_pairs, 2, nstate), conv_part
    )
    back_got = exchange(back, "doc")
    copies = call(
        functools.partial(total_body, pairs, state_pairs), shaped((parts, 8, nstate), F32), "v"
    )(back_got.reshape(-1, nstate))
    got = exchange(copies, "fsdp")
    grad_state, grad_conv = call(
        place_body,
        (shaped((slots, state_pairs, 2, nstate), BF16), shaped((slots, 1, 2, nstate), BF16)),
        "sv",
    )(carry_from, back_got)
    index = lax.axis_index("fsdp").astype(jnp.int32).reshape(1)
    grad_proj = call(
        final_body, shaped((model_width // (parts * slots), 2 * nstate), F32), "sv"
    )(index, got)
    grad_state = grad_state.reshape(carried_state.shape)
    grad_conv = grad_conv[:, 0, 0, : (taps - 1) * rows_in].reshape(carried_conv.shape)
    return (grad_proj, grad_state, grad_conv)


def solution(mesh):
    return jax.shard_map(
        shards,
        mesh=mesh,
        in_specs=(
            P("doc", None, None),
            P("doc", None, "fsdp"),
            P("doc", None, "fsdp"),
            P("doc", None),
            P("doc", None, "fsdp"),
            P("fsdp", None),
            P(None, "fsdp"),
            P("fsdp"),
            P(None, "fsdp", "doc", None),
            P(None, None, "fsdp", "doc"),
            P(),
        ),
        out_specs=(
            P(("doc", "fsdp"), None),
            P(None, "fsdp", "doc", None),
            P(None, None, "fsdp", "doc"),
        ),
        check_vma=False,
    )
```
